32 devices in a mesh: dp: 4 (over y, core), row: 2 (over x), col: 4 (over z).
Axes of the slice: x: 2, y: 2, z: 4, core: 2. Of those that a mesh axis runs over, the one named last changes fastest.
Arguments:
- hidden_in: bfloat16 [5120, 2048], P(('dp', 'col'), 'row'), may hold values from -6 to 6
- seq_lengths: int32 [4], P('dp'), may hold values from 512 to 1280, as said below
- gain_attn: bfloat16 [2048], P('row'), may hold values from 0.5 to 1.5
- w_query: bfloat16 [2048, 2048], P('row', 'col'), may hold values from -0.125 to 0.125
- w_key: bfloat16 [2048, 2048], P('row', 'col'), may hold values from -0.125 to 0.125
- w_value: bfloat16 [2048, 2048], P('row', 'col'), may hold values from -0.125 to 0.125
- w_outgate: bfloat16 [2048, 2048], P('row', 'col'), may hold values from -0.125 to 0.125
- rank_down: bfloat16 [2048, 16], P('row'), may hold values from -0.125 to 0.125
- rank_up: bfloat16 [16, 2048], P(None, 'col'), may hold values from -1.5 to 1.5
- decay_bias: float32 [2048], P('col'), may hold values from -1 to 7
- gain_head: bfloat16 [512], P('row'), may hold values from 0.5 to 1.5
- w_output: bfloat16 [2048, 2048], P('col', 'row'), may hold values from -0.1875 to 0.1875
- gain_ffn: bfloat16 [2048], P('row'), may hold values from 0.5 to 1.5
- w_gate: bfloat16 [2048, 5632], P('row', 'col'), may hold values from -0.125 to 0.125
- w_up: bfloat16 [2048, 5632], P('row', 'col'), may hold values from -0.125 to 0.125
- w_down: bfloat16 [5632, 2048], P('col', 'row'), may hold values from -0.109375 to 0.109375
- cotangent: bfloat16 [5120, 2048], P(('dp', 'col'), 'row'), may hold values from -6 to 6
Outputs:
- block_out: bfloat16 [5120, 2048], P(('dp', 'col'), 'row')
- grad_input: float32 [5120, 2048], P(('dp', 'col'), 'row')
- grad_gain_attn: float32 [2048], P('row')
- grad_w_query: float32 [2048, 2048], P('row', 'col')
- grad_w_key: float32 [2048, 2048], P('row', 'col')
- grad_w_value: float32 [2048, 2048], P('row', 'col')
- grad_w_outgate: float32 [2048, 2048], P('row', 'col')
- grad_rank_down: float32 [2048, 16], P('row')
- grad_rank_up: float32 [16, 2048], P(None, 'col')
- grad_decay_bias: float32 [2048], P('col')
- grad_gain_head: float32 [512], P('row')
- grad_w_output: float32 [2048, 2048], P('col', 'row')
- grad_gain_ffn: float32 [2048], P('row')
- grad_w_gate: float32 [2048, 5632], P('row', 'col')
- grad_w_up: float32 [2048, 5632], P('row', 'col')
- grad_w_down: float32 [5632, 2048], P('col', 'row')
The draws below stay inside these ranges and needn't reach their ends.
Inputs may be any that keep to these rules, and one draw needn't show every extreme that they name: `seq_lengths`: valid tokens of each slot of 1280 positions; every draw has one full slot and one slot of exactly 512 tokens.
All inputs are finite; a program needn't handle non-finite values.
Results may differ from the reference program's by a relative error of at most 0.025.
Values may be sent and summed in bfloat16 or wider, within the bound.
No kernel may reach another device: no remote copies, remote signals or barrier semaphores. Data moves between devices by JAX's collectives and lax.ppermute only.
A program may use at most 256 MiB of HBM per device.

```python
import math
import jax
import jax.numpy as jnp
from jax import lax

D = 2048
HEADS = 4
HEAD_K = 512
HEAD_V = 512
FF = 5632
RANK = 16
BLOCK = 64
SLOT = 1280
MIN_LEN = 512
SEQS = 4
TOKENS = 5120


def draw_seq_lengths(key, part):
    lengths = jax.random.randint(key, (SEQS,), MIN_LEN, SLOT + 1)
    chosen = jax.random.randint(jax.random.fold_in(key, 7), (), 0, SEQS)
    places = jnp.arange(SEQS)
    lengths = jnp.where(places == chosen, SLOT, lengths)
    lengths = jnp.where(places == (chosen + 1) % SEQS, MIN_LEN, lengths)
    return lengths.astype(jnp.int32)


def level_of(own_key, shape, pieces, smallest, top_value):
    def one(dim, blocks):
        draws = jax.random.uniform(jax.random.fold_in(jax.random.fold_in(own_key, 6), dim), (blocks,), jnp.float32, smallest / len(pieces), top_value / len(pieces))
        return jnp.repeat(jnp.exp(draws), shape[dim] // blocks).reshape((-1,) + (1,) * (len(shape) - dim - 1))

    loudness = one(*pieces[0])
    for cut in pieces[1:]:
        loudness = loudness * one(*cut)
    return loudness


def noise(own_key, shape, width, bound, shards=(), held_as=jnp.bfloat16):
    level = level_of(own_key, shape, shards, -0.22, 0.18) if shards else 1.0
    drawn = jax.random.normal(own_key, shape, jnp.float32) * width * level
    return jnp.minimum(jnp.maximum(drawn, -bound), bound).astype(held_as)


def setup_inputs(seed: int = 0) -> dict:
    key_list = jax.random.split(jax.random.key(seed), 18)
    hidden_in = noise(key_list[0], (TOKENS, D), 1.0, 6.0, ((0, 16), (1, 2)))
    seq_lengths = draw_seq_lengths(jax.random.fold_in(key_list[17], 71), 0)
    gain_attn = jnp.clip(1.0 + 0.1 * jax.random.normal(key_list[2], (D,), jnp.float32), 0.5, 1.5).astype(jnp.bfloat16)
    w_query = noise(key_list[3], (D, HEADS * HEAD_K), D ** -0.5, 0.125, ((0, 2), (1, 4)))
    w_key = noise(key_list[4], (D, HEADS * HEAD_K), D ** -0.5, 0.125, ((0, 2), (1, 4)))
    w_value = noise(key_list[5], (D, HEADS * HEAD_V), D ** -0.5, 0.125, ((0, 2), (1, 4)))
    w_outgate = noise(key_list[6], (D, HEADS * HEAD_V), D ** -0.5, 0.125, ((0, 2), (1, 4)))
    rank_down = noise(key_list[7], (D, RANK), D ** -0.5, 0.125, ((0, 2),))
    rank_up = noise(key_list[8], (RANK, HEADS * HEAD_K), RANK ** -0.5, 1.5, ((1, 4),))
    decay_bias = jnp.clip(-1.0 + 8.0 * jax.random.uniform(key_list[9], (HEADS * HEAD_K,), jnp.float32) ** level_of(key_list[9], (HEADS * HEAD_K,), ((0, 4),), -0.2, 0.2), -1.0, 7.0)
    gain_head = jnp.clip(1.0 + 0.1 * jax.random.normal(key_list[10], (HEAD_V,), jnp.float32), 0.5, 1.5).astype(jnp.bfloat16)
    w_output = noise(key_list[11], (HEADS * HEAD_V, D), (HEADS * HEAD_V // 2) ** -0.5, 0.1875, ((0, 4), (1, 2)))
    gain_ffn = jnp.clip(1.0 + 0.1 * jax.random.normal(key_list[12], (D,), jnp.float32), 0.5, 1.5).astype(jnp.bfloat16)
    w_gate = noise(key_list[13], (D, FF), D ** -0.5, 0.125, ((0, 2), (1, 4)))
    w_up = noise(key_list[14], (D, FF), D ** -0.5, 0.125, ((0, 2), (1, 4)))
    w_down = noise(key_list[15], (FF, D), (FF // 2) ** -0.5, 0.109375, ((0, 4), (1, 2)))
    cotangent = noise(key_list[16], (TOKENS, D), 1.0, 6.0, ((0, 16), (1, 2)))
    return {"hidden_in": hidden_in, "seq_lengths": seq_lengths, "gain_attn": gain_attn, "w_query": w_query, "w_key": w_key, "w_value": w_value, "w_outgate": w_outgate, "rank_down": rank_down, "rank_up": rank_up, "decay_bias": decay_bias, "gain_head": gain_head, "w_output": w_output, "gain_ffn": gain_ffn, "w_gate": w_gate, "w_up": w_up, "w_down": w_down, "cotangent": cotangent}


@jax.custom_vjp
def low(v):
    return lax.optimization_barrier(v.astype(jnp.bfloat16)).astype(jnp.float32)

@jax.custom_vjp
def low_back(v):
    return v

def low_keep(v):
    return (low(v), None)

def low_pass(kept, grad):
    return (grad,)

def back_keep(v):
    return (v, None)

def back_low(kept, grad):
    return (low(grad),)
low.defvjp(low_keep, low_pass)
low_back.defvjp(back_keep, back_low)
EPSILON = 1e-06
HIGHEST = lax.Precision.HIGHEST

def matmul(left, right):
    return jnp.dot(left, right, precision=HIGHEST, preferred_element_type=jnp.float32)

def rms_scale(values, gains):
    return values * lax.rsqrt(lax.optimization_barrier(jnp.mean(values * values, axis=-1, keepdims=True)) + EPSILON) * gains

def gla_sequence(queries, key_rows, value_rows, decays):
    block_count = queries.shape[0] // BLOCK
    key_extent = queries.shape[1]
    value_extent = value_rows.shape[1]
    query_blocks = queries.reshape(block_count, BLOCK, key_extent)
    key_blocks = key_rows.reshape(block_count, BLOCK, key_extent)
    value_blocks = value_rows.reshape(block_count, BLOCK, value_extent)
    decay_blocks = decays.reshape(block_count, BLOCK, key_extent)
    running = jnp.cumsum(decay_blocks, axis=1)
    ending = running[:, -1:, :]
    query_fade = query_blocks * jnp.exp(running)
    key_grow = key_blocks * jnp.exp(-running)
    key_final = key_blocks * jnp.exp(ending - running)
    causal = jnp.tril(jnp.ones((BLOCK, BLOCK), jnp.float32))
    scores = jnp.einsum('bik,bjk->bij', query_fade, key_grow, precision=HIGHEST) * causal
    within = jnp.einsum('bij,bjv->biv', scores, value_blocks, precision=HIGHEST)
    updates = jnp.einsum('bjk,bjv->bkv', key_final, value_blocks, precision=HIGHEST)
    fading = jnp.exp(ending[:, 0, :])

    def advance(carried, inputs_now):
        update_now, fade_now = inputs_now
        return (carried * fade_now[:, None] + update_now, carried)
    initial = jnp.zeros((key_extent, value_extent), jnp.float32)
    _, earlier = lax.scan(advance, initial, (updates, fading))
    across = jnp.einsum('bik,bkv->biv', query_fade, earlier, precision=HIGHEST)
    return (within + across).reshape(block_count * BLOCK, value_extent)

def slot_forward(params, slot_input, slot_valid):
    gain_attn, w_query, w_key, w_value, w_outgate, rank_down, rank_up, decay_bias, gain_head, w_output, gain_ffn, w_gate, w_up, w_down = params
    positions = slot_input.shape[0]
    normed_one = low(rms_scale(slot_input, gain_attn))
    queries = low_back(low(matmul(normed_one, w_query)))
    key_rows = low_back(low(matmul(normed_one, w_key)))
    value_rows = low_back(low(matmul(normed_one, w_value)))
    outgate = low_back(matmul(normed_one, w_outgate))
    rank_mid = low_back(low(matmul(normed_one, rank_down)))
    decays = jax.nn.log_sigmoid(matmul(rank_mid, rank_up) + decay_bias) / 16.0
    scaled = queries * (1.0 / math.sqrt(HEAD_K))
    mixed = jax.vmap(gla_sequence, in_axes=1, out_axes=1)(scaled.reshape(positions, HEADS, HEAD_K), key_rows.reshape(positions, HEADS, HEAD_K), value_rows.reshape(positions, HEADS, HEAD_V), decays.reshape(positions, HEADS, HEAD_K))
    mixed = low_back(mixed)
    normed_head = rms_scale(mixed, gain_head).reshape(positions, HEADS * HEAD_V)
    gated = low(normed_head * jax.nn.silu(outgate))
    attn_out = low_back(matmul(gated, w_output))
    residual_mid = slot_input + attn_out
    normed_two = low(rms_scale(residual_mid, gain_ffn))
    gate_pre = low_back(matmul(normed_two, w_gate))
    up_pre = low_back(matmul(normed_two, w_up))
    hidden_act = low(jax.nn.silu(gate_pre) * up_pre)
    ffn_out = low_back(matmul(hidden_act, w_down))
    return slot_valid[:, None] * (residual_mid + ffn_out)

def reference(hidden_in, seq_lengths, gain_attn, w_query, w_key, w_value, w_outgate, rank_down, rank_up, decay_bias, gain_head, w_output, gain_ffn, w_gate, w_up, w_down, cotangent):
    params = tuple((tensor.astype(jnp.float32) for tensor in (gain_attn, w_query, w_key, w_value, w_outgate, rank_down, rank_up, decay_bias, gain_head, w_output, gain_ffn, w_gate, w_up, w_down)))
    slot_inputs = hidden_in.astype(jnp.float32).reshape(SEQS, SLOT, D)
    slot_seeds = cotangent.astype(jnp.float32).reshape(SEQS, SLOT, D)
    valid = (jnp.arange(SLOT)[None, :] < seq_lengths[:, None]).astype(jnp.float32)
    slot_step = jax.checkpoint(slot_forward)

    def forward(weights, inputs_all):

        def visit(carried, inputs_now):
            return (carried, slot_step(weights, inputs_now[0], inputs_now[1]))
        _, outputs = lax.scan(visit, jnp.zeros((), jnp.float32), (inputs_all, valid))
        return outputs
    outputs, pullback = jax.vjp(forward, params, slot_inputs)
    grads, input_grads = pullback(slot_seeds)
    return (outputs.reshape(SEQS * SLOT, D).astype(jnp.bfloat16), input_grads.reshape(SEQS * SLOT, D), grads[0], grads[1], grads[2], grads[3], grads[4], grads[5], grads[6], grads[7], grads[8], grads[9], grads[10], grads[11], grads[12], grads[13])
```

```python
import math

import jax
import jax.numpy as jnp
from jax import lax
from jax.experimental import pallas as pl
from jax.experimental.pallas import tpu as pltpu
from jax.sharding import PartitionSpec as P

HEAD_K = 512
HEAD_V = 512
SLOT = 1280
EPSILON = 1e-06
HIGHEST = lax.Precision.HIGHEST
HIGH = lax.Precision.HIGH
F32 = jnp.float32
BF16 = jnp.bfloat16

NN = (((1,), (0,)), ((), ()))
NT = (((1,), (1,)), ((), ()))
TN = (((0,), (0,)), ((), ()))


def dot(left, right, dims, precision=None):
    return lax.dot_general(left, right, dims, precision=precision, preferred_element_type=F32)


def split(x):
    high = x.astype(BF16)
    return (high, (x - high.astype(F32)).astype(BF16))


def split_three(x):
    high = x.astype(BF16)
    rest = x - high.astype(F32)
    middle = rest.astype(BF16)
    return (high, middle, (rest - middle.astype(F32)).astype(BF16))


def dot_pair(left, right, dims):
    return (
        dot(left[0], right[0], dims) + dot(left[0], right[1], dims) + dot(left[1], right[0], dims)
    )


def dot_left(left, right, dims):
    return dot(left[0], right, dims) + dot(left[1], right, dims)


def dot_right(left, right, dims):
    return dot(left, right[0], dims) + dot(left, right[1], dims)


def lower_mask(size):
    rows = lax.broadcasted_iota(jnp.int32, (size, size), 0)
    cols = lax.broadcasted_iota(jnp.int32, (size, size), 1)
    return rows >= cols


def block_factors(q_ref, k_ref, decay_ref):
    size = q_ref.shape[0]
    causal = lower_mask(size)
    ones = jnp.where(causal, 1.0, 0.0).astype(BF16)
    parts = split_three(decay_ref[...])
    running = dot(ones, parts[0], NN) + dot(ones, parts[1], NN) + dot(ones, parts[2], NN)
    ending = running[size - 1 :, :]
    grow = jnp.exp(running)
    shrink = jnp.exp(-running)
    last = jnp.exp(ending - running)
    scale = 1.0 / math.sqrt(HEAD_K)
    keys = k_ref[...].astype(F32)
    query_fade = q_ref[...].astype(F32) * scale * grow
    return (causal, ones, ending, grow, shrink, last, query_fade, keys * shrink, keys * last)


def forward_kernel(
    q_ref, k_ref, v_ref, decay_ref, mixed_ref, faded_ref, state_ref, before_ref, carried, total
):
    @pl.when(pl.program_id(0) == 0)
    def _():
        carried[...] = jnp.zeros_like(carried)
        total[...] = jnp.zeros_like(total)

    causal, _, ending, _, _, _, query_fade, key_grow, key_final = block_factors(
        q_ref, k_ref, decay_ref
    )
    values = v_ref[...]
    state = carried[...]
    before = total[...]
    state_ref[0] = state
    before_ref[0] = before
    query_parts = split(query_fade)
    scores = jnp.where(causal, dot_pair(query_parts, split(key_grow), NT), 0.0)
    mixed_ref[...] = dot_left(split(scores), values, NN) + dot_pair(query_parts, split(state), NT)
    faded_ref[...] = query_fade * jnp.exp(before[:1, :])
    carried[...] = state * jnp.exp(ending) + dot_right(values, split(key_final), TN)
    total[...] = before + ending


def state_kernel(k_ref, v_ref, decay_ref, out_ref, carried):
    @pl.when(pl.program_id(0) == 0)
    def _():
        carried[...] = jnp.zeros_like(carried)

    _, _, ending, _, _, _, _, _, key_final = block_factors(k_ref, k_ref, decay_ref)
    state = carried[...] * jnp.exp(ending) + dot_right(v_ref[...], split(key_final), TN)
    carried[...] = state
    out_ref[...] = state


def backward_kernel(
    q_ref,
    k_ref,
    v_ref,
    decay_ref,
    grad_ref,
    state_ref,
    before_ref,
    entry_ref,
    exit_ref,
    query_out,
    key_out,
    value_out,
    decay_out,
    carried,
):
    @pl.when(pl.program_id(0) == 0)
    def _():
        carried[...] = exit_ref[...]

    causal, ones, ending, grow, shrink, last, query_fade, key_grow, key_final = block_factors(
        q_ref, k_ref, decay_ref
    )
    values = v_ref[...]
    state = state_ref[0] + jnp.exp(before_ref[0][:1, :]) * entry_ref[...]
    state_grad = carried[...]
    query_parts = split(query_fade)
    key_parts = split(key_grow)
    grad_parts = split(grad_ref[...])
    carry_parts = split(state_grad)
    scores = jnp.where(causal, dot_pair(query_parts, key_parts, NT), 0.0)
    score_grad = jnp.where(causal, dot_left(grad_parts, values, NT), 0.0)
    score_parts = split(score_grad)
    fade_grad = dot_pair(score_parts, key_parts, NN) + dot_pair(grad_parts, split(state), NN)
    grow_grad = dot_pair(score_parts, query_parts, TN)
    final_grad = dot_right(values, carry_parts, NN)
    value_out[...] = (
        dot_pair(split(scores), grad_parts, TN) + dot_pair(split(key_final), carry_parts, NT)
    ).astype(BF16)
    fading = jnp.exp(ending)
    carried[...] = fading * state_grad + dot_pair(grad_parts, query_parts, TN)
    query_out[...] = (fade_grad * grow * (1.0 / math.sqrt(HEAD_K))).astype(BF16)
    key_out[...] = (grow_grad * shrink + final_grad * last).astype(BF16)
    ended = final_grad * key_final
    running_grad = fade_grad * query_fade - grow_grad * key_grow - ended
    end_grad = jnp.sum(ended, axis=0, keepdims=True) + fading * jnp.sum(
        state_grad * state, axis=0, keepdims=True
    )
    parts = split_three(running_grad)
    decay_out[...] = (
        dot(ones, parts[0], TN) + dot(ones, parts[1], TN) + dot(ones, parts[2], TN) + end_grad
    )


def block_of(rows):
    return 64 if rows % 64 == 0 else 32


def row_spec(block, width, count, backward):
    if backward:
        return pl.BlockSpec((block, width), lambda b: (count - 1 - b, 0))
    return pl.BlockSpec((block, width), lambda b: (b, 0))


def cube_spec(height, width, count, backward):
    if backward:
        return pl.BlockSpec((1, height, width), lambda b: (count - 1 - b, 0, 0))
    return pl.BlockSpec((1, height, width), lambda b: (b, 0, 0))


def kernel_params():
    return pltpu.CompilerParams(dimension_semantics=("arbitrary",))


def attend_forward(queries, keys, values, decays):
    rows = queries.shape[0]
    block = block_of(rows)
    count = rows // block
    row_k = row_spec(block, HEAD_K, count, False)
    row_v = row_spec(block, HEAD_V, count, False)
    return pl.pallas_call(
        forward_kernel,
        grid=(count,),
        in_specs=[row_k, row_k, row_v, row_k],
        out_specs=[
            row_v,
            row_k,
            cube_spec(HEAD_V, HEAD_K, count, False),
            cube_spec(8, HEAD_K, count, False),
        ],
        out_shape=[
            jax.ShapeDtypeStruct((rows, HEAD_V), F32),
            jax.ShapeDtypeStruct((rows, HEAD_K), F32),
            jax.ShapeDtypeStruct((count, HEAD_V, HEAD_K), F32),
            jax.ShapeDtypeStruct((count, 8, HEAD_K), F32),
        ],
        scratch_shapes=[pltpu.VMEM((HEAD_V, HEAD_K), F32), pltpu.VMEM((8, HEAD_K), F32)],
        compiler_params=kernel_params(),
        name="recurrence_forward",
    )(queries, keys, values, decays)


def attend_state(keys, values, decays):
    rows = keys.shape[0]
    block = block_of(rows)
    count = rows // block
    row_k = row_spec(block, HEAD_K, count, False)
    row_v = row_spec(block, HEAD_V, count, False)
    return pl.pallas_call(
        state_kernel,
        grid=(count,),
        in_specs=[row_k, row_v, row_k],
        out_specs=pl.BlockSpec((HEAD_V, HEAD_K), lambda b: (0, 0)),
        out_shape=jax.ShapeDtypeStruct((HEAD_V, HEAD_K), F32),
        scratch_shapes=[pltpu.VMEM((HEAD_V, HEAD_K), F32)],
        compiler_params=kernel_params(),
        name="recurrence_state",
    )(keys, values, decays)


def attend_backward(queries, keys, values, decays, grads, states, before, entry, exit_grad):
    rows = queries.shape[0]
    block = block_of(rows)
    count = rows // block
    row_k = row_spec(block, HEAD_K, count, True)
    row_v = row_spec(block, HEAD_V, count, True)
    whole = pl.BlockSpec((HEAD_V, HEAD_K), lambda b: (0, 0))
    return pl.pallas_call(
        backward_kernel,
        grid=(count,),
        in_specs=[
            row_k,
            row_k,
            row_v,
            row_k,
            row_v,
            cube_spec(HEAD_V, HEAD_K, count, True),
            cube_spec(8, HEAD_K, count, True),
            whole,
            whole,
        ],
        out_specs=[row_k, row_k, row_v, row_k],
        out_shape=[
            jax.ShapeDtypeStruct((rows, HEAD_K), BF16),
            jax.ShapeDtypeStruct((rows, HEAD_K), BF16),
            jax.ShapeDtypeStruct((rows, HEAD_V), BF16),
            jax.ShapeDtypeStruct((rows, HEAD_K), F32),
        ],
        scratch_shapes=[pltpu.VMEM((HEAD_V, HEAD_K), F32)],
        compiler_params=kernel_params(),
        name="recurrence_backward",
    )(queries, keys, values, decays, grads, states, before, entry, exit_grad)


class Place:
    def __init__(self):
        self.rows = lax.axis_size("row")
        self.cols = lax.axis_size("col")
        self.groups = lax.axis_size("dp")
        self.row = lax.axis_index("row")
        self.col = lax.axis_index("col")
        self.group = lax.axis_index("dp")

    def from_row(self, x, step):
        n = self.rows
        return lax.ppermute(x, "row", [((i + step) % n, i) for i in range(n)])

    def to_row(self, x, step):
        n = self.rows
        return lax.ppermute(x, "row", [(i, (i + step) % n) for i in range(n)])

    def swap_group(self, x, bit):
        return lax.ppermute(x, "dp", [(i, i ^ bit) for i in range(self.groups)])

    def home_pairs(self, k):
        pairs = []
        for x in range(self.rows):
            for z in range(self.cols):
                slot = (x - k) % self.rows
                place = z * self.rows + slot
                pairs.append((x * self.cols + z, place))
        return pairs

    def to_home(self, x):
        high = x.shape[0] // self.rows
        wide = x.shape[1]
        out = jnp.zeros((high, wide * self.rows), x.dtype)
        own_slot = (self.row * self.cols + self.col) % self.rows
        for k in range(self.rows):
            slot = (self.row - k) % self.rows
            piece = lax.dynamic_slice_in_dim(x, slot * high, high, 0)
            piece = lax.ppermute(piece, ("row", "col"), self.home_pairs(k))
            at = (own_slot + k - self.row) % self.rows
            out = lax.dynamic_update_slice_in_dim(out, piece, at * wide, 1)
        return out

    def from_home(self, y):
        high = y.shape[0]
        wide = y.shape[1] // self.rows
        out = jnp.zeros((high * self.rows, wide), y.dtype)
        own_slot = (self.row * self.cols + self.col) % self.rows
        for k in range(self.rows):
            at = (own_slot + k - self.row) % self.rows
            piece = lax.dynamic_slice_in_dim(y, at * wide, wide, 1)
            pairs = [(home, first) for first, home in self.home_pairs(k)]
            piece = lax.ppermute(piece, ("row", "col"), pairs)
            slot = (self.row - k) % self.rows
            out = lax.dynamic_update_slice_in_dim(out, piece, slot * high, 0)
        return out

    def join(self, mine, other, bit):
        high = (self.group & bit) != 0
        return jnp.concatenate([jnp.where(high, other, mine), jnp.where(high, mine, other)], axis=0)

    def blocks_of(self, own):
        blocks = [own]
        high = own.shape[0] // self.groups
        share = lax.dynamic_slice_in_dim(own, self.group * high, high, 0)
        for step in range(1, self.rows):
            part = self.from_row(share, step)
            bit = 1
            while bit < self.groups:
                part = self.join(part, self.swap_group(part, bit), bit)
                bit *= 2
            blocks.append(part)
        return blocks

    def halves(self, x):
        wide = x.shape[1] // 2
        bit = self.group & 1
        keep = lax.dynamic_slice_in_dim(x, bit * wide, wide, 1)
        send = lax.dynamic_slice_in_dim(x, (1 - bit) * wide, wide, 1)
        return (keep, send)

    def reduce_weight(self, product):
        sent = [self.swap_group(part.astype(BF16), 1) for part in product("send")]
        kept = product("keep")
        summed = [a + b.astype(F32) for a, b in zip(kept, sent)]
        own = summed[0]
        for step in range(1, self.rows):
            own = own + self.to_row(summed[step].astype(BF16), step).astype(F32)
        bit = 2
        while bit < self.groups:
            high = own.shape[0] // 2
            side = jnp.where((self.group & bit) != 0, 1, 0)
            keep = lax.dynamic_slice_in_dim(own, side * high, high, 0)
            send = lax.dynamic_slice_in_dim(own, (1 - side) * high, high, 0)
            own = keep + self.swap_group(send.astype(BF16), bit).astype(F32)
            bit *= 2
        own = own.astype(BF16)
        bit //= 2
        while bit >= 1:
            own = self.join(own, self.swap_group(own, bit), bit)
            bit //= 2
        return own.astype(F32)


def gather_tokens(x):
    return lax.all_gather(x, "col", axis=0, tiled=True)


def scatter_tokens(parts):
    return lax.psum_scatter(
        jnp.concatenate([part.astype(BF16) for part in parts], axis=1),
        "col",
        scatter_dimension=0,
        tiled=True,
    ).astype(F32)


def columns(x, count):
    wide = x.shape[1] // count
    return [x[:, i * wide : (i + 1) * wide] for i in range(count)]


def over_features(parts, blocks):
    total = dot(parts[0], blocks[0], NN)
    for part, block in zip(parts[1:], blocks[1:]):
        total = total + dot(part, block, NN)
    return total


def over_features_back(parts, blocks):
    total = dot(parts[0], blocks[0], NT)
    for part, block in zip(parts[1:], blocks[1:]):
        total = total + dot(part, block, NT)
    return total


def norm_factor(values):
    return lax.rsqrt(jnp.mean(values * values, axis=1, keepdims=True) + EPSILON)


def norm_backward(values, factor, gains, upstream):
    weighted = upstream * gains
    inner = jnp.sum(weighted * values, axis=1, keepdims=True)
    grad_values = factor * weighted - values * (
        factor * factor * factor * inner / values.shape[1]
    )
    return (grad_values, jnp.sum(upstream * values * factor, axis=0))


def body(
    hidden_in,
    seq_lengths,
    gain_attn,
    w_query,
    w_key,
    w_value,
    w_outgate,
    rank_down,
    rank_up,
    decay_bias,
    gain_head,
    w_output,
    gain_ffn,
    w_gate,
    w_up,
    w_down,
    cotangent,
):
    place = Place()
    rows, cols = place.rows, place.cols
    half_rows = SLOT // rows
    home_rows = half_rows // cols
    wide = hidden_in.shape[1]
    rank = rank_down.shape[1]
    head_wide = gain_head.shape[0]

    residual_in = place.to_home(hidden_in).astype(F32)
    w_in = jnp.concatenate([w_query, w_key, w_value, w_outgate], axis=1)
    w_two = jnp.concatenate([w_gate, w_up], axis=1)
    in_blocks = place.blocks_of(w_in)
    small = jnp.concatenate([gain_attn, gain_ffn, gain_head, rank_down.reshape(-1)])
    smalls = [small] + [place.from_row(small, step) for step in range(1, rows)]
    gain_one = jnp.concatenate([s[:wide] for s in smalls]).astype(F32)
    gain_two = jnp.concatenate([s[wide : 2 * wide] for s in smalls]).astype(F32)
    heads = jnp.stack([s[2 * wide : 2 * wide + head_wide] for s in smalls])
    gain_mix = jnp.roll(heads, place.row, axis=0).reshape(-1).astype(F32)
    down_blocks = [s[2 * wide + head_wide :].reshape(wide, rank) for s in smalls]

    place_home = place.row * half_rows + place.col * home_rows
    valid = (place_home + jnp.arange(home_rows) < seq_lengths[0]).astype(F32)[:, None]

    factor_one = norm_factor(residual_in)
    normed_one = (residual_in * factor_one * gain_one).astype(BF16)
    tokens_one = gather_tokens(normed_one)
    ones = columns(tokens_one, rows)
    pre = over_features(ones, in_blocks)
    queries = pre[:, :HEAD_K].astype(BF16)
    keys = pre[:, HEAD_K : 2 * HEAD_K].astype(BF16)
    values = pre[:, 2 * HEAD_K : 2 * HEAD_K + HEAD_V].astype(BF16)
    outgate = pre[:, 2 * HEAD_K + HEAD_V :]
    rank_mid = over_features(ones, down_blocks).astype(BF16)
    decay_logits = dot(rank_mid, rank_up, NN) + decay_bias
    decays = jax.nn.log_sigmoid(decay_logits) / 16.0

    ending = attend_state(keys, values, decays)
    steps = [(i, i + 1) for i in range(rows - 1)]
    entry = lax.ppermute(ending, "row", steps)
    if rows > 2:
        all_fade = jnp.exp(jnp.sum(decays, axis=0))[None, :]
        for _ in range(rows - 2):
            entry = lax.ppermute(entry * all_fade + ending, "row", steps)
    mixed, faded, states, before = attend_forward(queries, keys, values, decays)
    mixed = mixed + dot(faded, entry, NT, HIGH)
    factor_head = norm_factor(mixed)
    normed_head = mixed * factor_head * gain_mix
    out_sig = jax.nn.sigmoid(outgate)
    out_act = outgate * out_sig
    gated = (normed_head * out_act).astype(BF16)
    out_blocks = place.blocks_of(w_output)
    attn_out = scatter_tokens([dot(gated, block, NN) for block in out_blocks])
    residual_mid = residual_in + attn_out

    factor_two = norm_factor(residual_mid)
    normed_two = (residual_mid * factor_two * gain_two).astype(BF16)
    tokens_two = gather_tokens(normed_two)
    twos = columns(tokens_two, rows)
    two_blocks = place.blocks_of(w_two)
    both = over_features(twos, two_blocks)
    hidden_wide = w_gate.shape[1]
    gate_pre = both[:, :hidden_wide]
    up_pre = both[:, hidden_wide:]
    swish_sig = jax.nn.sigmoid(gate_pre)
    swish_out = gate_pre * swish_sig
    hidden = (swish_out * up_pre).astype(BF16)
    ffn_blocks = place.blocks_of(w_down)

    upstream = valid * place.to_home(cotangent).astype(F32)
    ffn_grad = gather_tokens(upstream.astype(BF16))
    ffn_grads = columns(ffn_grad, rows)
    hidden_grad = over_features_back(ffn_grads, ffn_blocks)
    swish_slope = swish_sig * (1.0 + gate_pre * (1.0 - swish_sig))
    gate_grad = (hidden_grad * up_pre * swish_slope).astype(BF16)
    up_grad = (hidden_grad * swish_out).astype(BF16)
    both_grad = jnp.concatenate([gate_grad, up_grad], axis=1)

    normed_two_grad = scatter_tokens([dot(both_grad, block, NT) for block in two_blocks])
    mid_part, gain_two_grad = norm_backward(residual_mid, factor_two, gain_two, normed_two_grad)
    mid_grad = upstream + mid_part
    ffn_out = scatter_tokens([dot(hidden, block, NN) for block in ffn_blocks])
    block_out = place.from_home((valid * (residual_mid + ffn_out)).astype(BF16))

    attn_grad = gather_tokens(mid_grad.astype(BF16))
    attn_grads = columns(attn_grad, rows)
    gated_grad = over_features_back(attn_grads, out_blocks)
    head_grad = gated_grad * out_act
    out_slope = out_sig * (1.0 + outgate * (1.0 - out_sig))
    outgate_grad = (gated_grad * normed_head * out_slope).astype(BF16)
    mixed_grad, gain_mix_grad = norm_backward(mixed, factor_head, gain_mix, head_grad)

    start_grad = dot(mixed_grad, faded, TN, HIGH)
    back = [(i + 1, i) for i in range(rows - 1)]
    exit_grad = lax.ppermute(start_grad, "row", back)
    if rows > 2:
        for _ in range(rows - 2):
            exit_grad = lax.ppermute(exit_grad * all_fade + start_grad, "row", back)
    query_grad, key_grad, value_grad, decay_grad = attend_backward(
        queries, keys, values, decays, mixed_grad, states, before, entry, exit_grad
    )
    logit_grad = decay_grad * jax.nn.sigmoid(-decay_logits) / 16.0
    rank_up_part = dot(rank_mid.astype(F32), logit_grad, TN, HIGHEST)
    bias_part = jnp.sum(logit_grad, axis=0)
    rank_term = dot(logit_grad, rank_up.astype(F32), NT, HIGHEST)
    rank_grad = lax.psum(rank_term, "col").astype(BF16)
    in_grad = jnp.concatenate([query_grad, key_grad, value_grad, outgate_grad], axis=1)
    normed_one_grad = scatter_tokens([dot(in_grad, block, NT) for block in in_blocks])
    own_rank = lax.dynamic_slice_in_dim(rank_grad, place.col * home_rows, home_rows, 0)
    normed_one_grad = normed_one_grad + jnp.concatenate(
        [dot(own_rank, block, NT) for block in down_blocks], axis=1
    )
    input_part, gain_one_grad = norm_backward(residual_in, factor_one, gain_one, normed_one_grad)
    grad_input = place.from_home((mid_grad + input_part).astype(BF16)).astype(F32)

    def tall(tokens, grads):
        def product(which):
            pick = 0 if which == "keep" else 1
            return [dot(place.halves(x)[pick], grads, TN) for x in columns(tokens, rows)]

        return place.reduce_weight(product)

    def broad(left, grads):
        def product(which):
            pick = 0 if which == "keep" else 1
            return columns(dot(place.halves(left)[pick], grads, TN), rows)

        return place.reduce_weight(product)

    grad_down = broad(hidden, ffn_grad)
    grad_two = tall(tokens_two, both_grad)
    grad_output = broad(gated, attn_grad)
    grad_in = tall(tokens_one, in_grad)

    def absolute(x):
        return jnp.roll(x.reshape((rows, -1) + x.shape[1:]), place.row, axis=0).reshape(x.shape)

    down_part = jnp.concatenate([dot(x, rank_grad, TN) for x in ones], axis=0)
    decay_all = lax.psum(
        (rank_up_part, bias_part, absolute(down_part)), ("dp", "row")
    )
    gains_all = lax.psum(
        (absolute(gain_one_grad), gain_mix_grad, absolute(gain_two_grad)), ("dp", "row", "col")
    )

    def mine(x):
        size = x.shape[0] // rows
        return lax.dynamic_slice_in_dim(x, place.row * size, size, 0)

    return (
        block_out,
        grad_input,
        mine(gains_all[0]),
        grad_in[:, :HEAD_K],
        grad_in[:, HEAD_K : 2 * HEAD_K],
        grad_in[:, 2 * HEAD_K : 2 * HEAD_K + HEAD_V],
        grad_in[:, 2 * HEAD_K + HEAD_V :],
        mine(decay_all[2]),
        decay_all[0],
        decay_all[1],
        mine(gains_all[1]),
        grad_output,
        mine(gains_all[2]),
        grad_two[:, :hidden_wide],
        grad_two[:, hidden_wide:],
        grad_down,
    )


def solution(mesh):
    placed = (
        P(("dp", "col"), "row"),
        P("dp"),
        P("row"),
        P("row", "col"),
        P("row", "col"),
        P("row", "col"),
        P("row", "col"),
        P("row", None),
        P(None, "col"),
        P("col"),
        P("row"),
        P("col", "row"),
        P("row"),
        P("row", "col"),
        P("row", "col"),
        P("col", "row"),
        P(("dp", "col"), "row"),
    )
    return jax.shard_map(
        body,
        mesh=mesh,
        in_specs=placed,
        out_specs=(
            P(("dp", "col"), "row"),
            P(("dp", "col"), "row"),
            P("row"),
            P("row", "col"),
            P("row", "col"),
            P("row", "col"),
            P("row", "col"),
            P("row", None),
            P(None, "col"),
            P("col"),
            P("row"),
            P("col", "row"),
            P("row"),
            P("row", "col"),
            P("row", "col"),
            P("col", "row"),
        ),
        check_vma=False,
    )
```

```python
import math

import jax
import jax.numpy as jnp
from jax import lax
from jax.experimental import pallas as pl
from jax.experimental.pallas import tpu as pltpu
from jax.sharding import PartitionSpec as P

HEAD_K = 512
HEAD_V = 512
SLOT = 1280
EPSILON = 1e-06
HIGHEST = lax.Precision.HIGHEST
HIGH = lax.Precision.HIGH
F32 = jnp.float32
BF16 = jnp.bfloat16

NN = (((1,), (0,)), ((), ()))
NT = (((1,), (1,)), ((), ()))
TN = (((0,), (0,)), ((), ()))


def dot(left, right, dims, precision=None):
    return lax.dot_general(left, right, dims, precision=precision, preferred_element_type=F32)


def split(x):
    high = x.astype(BF16)
    return (high, (x - high.astype(F32)).astype(BF16))


def split_three(x):
    high = x.astype(BF16)
    rest = x - high.astype(F32)
    middle = rest.astype(BF16)
    return (high, middle, (rest - middle.astype(F32)).astype(BF16))


def dot_pair(left, right, dims):
    return (
        dot(left[0], right[0], dims) + dot(left[0], right[1], dims) + dot(left[1], right[0], dims)
    )


def dot_left(left, right, dims):
    return dot(left[0], right, dims) + dot(left[1], right, dims)


def dot_right(left, right, dims):
    return dot(left, right[0], dims) + dot(left, right[1], dims)


def lower_mask(size):
    rows = lax.broadcasted_iota(jnp.int32, (size, size), 0)
    cols = lax.broadcasted_iota(jnp.int32, (size, size), 1)
    return rows >= cols


def block_factors(q_ref, k_ref, decay_ref):
    size = q_ref.shape[0]
    causal = lower_mask(size)
    ones = jnp.where(causal, 1.0, 0.0).astype(BF16)
    parts = split_three(decay_ref[...])
    running = dot(ones, parts[0], NN) + dot(ones, parts[1], NN) + dot(ones, parts[2], NN)
    ending = running[size - 1 :, :]
    grow = jnp.exp(running)
    shrink = jnp.exp(-running)
    last = jnp.exp(ending - running)
    scale = 1.0 / math.sqrt(HEAD_K)
    keys = k_ref[...].astype(F32)
    query_fade = q_ref[...].astype(F32) * scale * grow
    return (causal, ones, ending, grow, shrink, last, query_fade, keys * shrink, keys * last)


def forward_kernel(
    q_ref, k_ref, v_ref, decay_ref, mixed_ref, faded_ref, state_ref, before_ref, carried, total
):
    @pl.when(pl.program_id(0) == 0)
    def _():
        carried[...] = jnp.zeros_like(carried)
        total[...] = jnp.zeros_like(total)

    causal, _, ending, _, _, _, query_fade, key_grow, key_final = block_factors(
        q_ref, k_ref, decay_ref
    )
    values = v_ref[...]
    state = carried[...]
    before = total[...]
    state_ref[0] = state
    before_ref[0] = before
    query_parts = split(query_fade)
    scores = jnp.where(causal, dot_pair(query_parts, split(key_grow), NT), 0.0)
    mixed_ref[...] = dot_left(split(scores), values, NN) + dot_pair(query_parts, split(state), NT)
    faded_ref[...] = query_fade * jnp.exp(before[:1, :])
    carried[...] = state * jnp.exp(ending) + dot_right(values, split(key_final), TN)
    total[...] = before + ending


def state_kernel(k_ref, v_ref, decay_ref, out_ref, carried):
    @pl.when(pl.program_id(0) == 0)
    def _():
        carried[...] = jnp.zeros_like(carried)

    _, _, ending, _, _, _, _, _, key_final = block_factors(k_ref, k_ref, decay_ref)
    state = carried[...] * jnp.exp(ending) + dot_right(v_ref[...], split(key_final), TN)
    carried[...] = state
    out_ref[...] = state


def backward_kernel(
    q_ref,
    k_ref,
    v_ref,
    decay_ref,
    grad_ref,
    state_ref,
    before_ref,
    entry_ref,
    exit_ref,
    query_out,
    key_out,
    value_out,
    decay_out,
    carried,
):
    @pl.when(pl.program_id(0) == 0)
    def _():
        carried[...] = exit_ref[...]

    causal, ones, ending, grow, shrink, last, query_fade, key_grow, key_final = block_factors(
        q_ref, k_ref, decay_ref
    )
    values = v_ref[...]
    state = state_ref[0] + jnp.exp(before_ref[0][:1, :]) * entry_ref[...]
    state_grad = carried[...]
    query_parts = split(query_fade)
    key_parts = split(key_grow)
    grad_parts = split(grad_ref[...])
    carry_parts = split(state_grad)
    scores = jnp.where(causal, dot_pair(query_parts, key_parts, NT), 0.0)
    score_grad = jnp.where(causal, dot_left(grad_parts, values, NT), 0.0)
    score_parts = split(score_grad)
    fade_grad = dot_pair(score_parts, key_parts, NN) + dot_pair(grad_parts, split(state), NN)
    grow_grad = dot_pair(score_parts, query_parts, TN)
    final_grad = dot_right(values, carry_parts, NN)
    value_out[...] = (
        dot_pair(split(scores), grad_parts, TN) + dot_pair(split(key_final), carry_parts, NT)
    ).astype(BF16)
    fading = jnp.exp(ending)
    carried[...] = fading * state_grad + dot_pair(grad_parts, query_parts, TN)
    query_out[...] = (fade_grad * grow * (1.0 / math.sqrt(HEAD_K))).astype(BF16)
    key_out[...] = (grow_grad * shrink + final_grad * last).astype(BF16)
    ended = final_grad * key_final
    running_grad = fade_grad * query_fade - grow_grad * key_grow - ended
    end_grad = jnp.sum(ended, axis=0, keepdims=True) + fading * jnp.sum(
        state_grad * state, axis=0, keepdims=True
    )
    parts = split_three(running_grad)
    decay_out[...] = (
        dot(ones, parts[0], TN) + dot(ones, parts[1], TN) + dot(ones, parts[2], TN) + end_grad
    )


def block_of(rows):
    return 64 if rows % 64 == 0 else 32


def row_spec(block, width, count, backward):
    if backward:
        return pl.BlockSpec((block, width), lambda b: (count - 1 - b, 0))
    return pl.BlockSpec((block, width), lambda b: (b, 0))


def cube_spec(height, width, count, backward):
    if backward:
        return pl.BlockSpec((1, height, width), lambda b: (count - 1 - b, 0, 0))
    return pl.BlockSpec((1, height, width), lambda b: (b, 0, 0))


def kernel_params():
    return pltpu.CompilerParams(dimension_semantics=("arbitrary",))


def attend_forward(queries, keys, values, decays):
    rows = queries.shape[0]
    block = block_of(rows)
    count = rows // block
    row_k = row_spec(block, HEAD_K, count, False)
    row_v = row_spec(block, HEAD_V, count, False)
    return pl.pallas_call(
        forward_kernel,
        grid=(count,),
        in_specs=[row_k, row_k, row_v, row_k],
        out_specs=[
            row_v,
            row_k,
            cube_spec(HEAD_V, HEAD_K, count, False),
            cube_spec(8, HEAD_K, count, False),
        ],
        out_shape=[
            jax.ShapeDtypeStruct((rows, HEAD_V), F32),
            jax.ShapeDtypeStruct((rows, HEAD_K), F32),
            jax.ShapeDtypeStruct((count, HEAD_V, HEAD_K), F32),
            jax.ShapeDtypeStruct((count, 8, HEAD_K), F32),
        ],
        scratch_shapes=[pltpu.VMEM((HEAD_V, HEAD_K), F32), pltpu.VMEM((8, HEAD_K), F32)],
        compiler_params=kernel_params(),
        name="recurrence_forward",
    )(queries, keys, values, decays)


def attend_state(keys, values, decays):
    rows = keys.shape[0]
    block = block_of(rows)
    count = rows // block
    row_k = row_spec(block, HEAD_K, count, False)
    row_v = row_spec(block, HEAD_V, count, False)
    return pl.pallas_call(
        state_kernel,
        grid=(count,),
        in_specs=[row_k, row_v, row_k],
        out_specs=pl.BlockSpec((HEAD_V, HEAD_K), lambda b: (0, 0)),
        out_shape=jax.ShapeDtypeStruct((HEAD_V, HEAD_K), F32),
        scratch_shapes=[pltpu.VMEM((HEAD_V, HEAD_K), F32)],
        compiler_params=kernel_params(),
        name="recurrence_state",
    )(keys, values, decays)


def attend_backward(queries, keys, values, decays, grads, states, before, entry, exit_grad):
    rows = queries.shape[0]
    block = block_of(rows)
    count = rows // block
    row_k = row_spec(block, HEAD_K, count, True)
    row_v = row_spec(block, HEAD_V, count, True)
    whole = pl.BlockSpec((HEAD_V, HEAD_K), lambda b: (0, 0))
    return pl.pallas_call(
        backward_kernel,
        grid=(count,),
        in_specs=[
            row_k,
            row_k,
            row_v,
            row_k,
            row_v,
            cube_spec(HEAD_V, HEAD_K, count, True),
            cube_spec(8, HEAD_K, count, True),
            whole,
            whole,
        ],
        out_specs=[row_k, row_k, row_v, row_k],
        out_shape=[
            jax.ShapeDtypeStruct((rows, HEAD_K), BF16),
            jax.ShapeDtypeStruct((rows, HEAD_K), BF16),
            jax.ShapeDtypeStruct((rows, HEAD_V), BF16),
            jax.ShapeDtypeStruct((rows, HEAD_K), F32),
        ],
        scratch_shapes=[pltpu.VMEM((HEAD_V, HEAD_K), F32)],
        compiler_params=kernel_params(),
        name="recurrence_backward",
    )(queries, keys, values, decays, grads, states, before, entry, exit_grad)


def after(value, *others):
    return lax.optimization_barrier((value, others))[0]


class Place:
    def __init__(self):
        self.rows = lax.axis_size("row")
        self.cols = lax.axis_size("col")
        self.groups = lax.axis_size("dp")
        self.row = lax.axis_index("row")
        self.col = lax.axis_index("col")
        self.group = lax.axis_index("dp")

    def from_row(self, x, step):
        n = self.rows
        return lax.ppermute(x, "row", [((i + step) % n, i) for i in range(n)])

    def to_row(self, x, step):
        n = self.rows
        return lax.ppermute(x, "row", [(i, (i + step) % n) for i in range(n)])

    def swap(self, x, axis, bit):
        return lax.ppermute(x, axis, [(i, i ^ bit) for i in range(lax.axis_size(axis))])

    def sum_over(self, x, *axes):
        for axis in axes:
            bit = 1
            while bit < lax.axis_size(axis):
                x = x + self.swap(x, axis, bit)
                bit *= 2
        return x

    def home_pairs(self, k):
        pairs = []
        for x in range(self.rows):
            for z in range(self.cols):
                slot = (x - k) % self.rows
                place = z * self.rows + slot
                pairs.append((x * self.cols + z, place))
        return pairs

    def to_home(self, x):
        high = x.shape[0] // self.rows
        wide = x.shape[1]
        out = jnp.zeros((high, wide * self.rows), x.dtype)
        own_slot = (self.row * self.cols + self.col) % self.rows
        for k in range(self.rows):
            slot = (self.row - k) % self.rows
            piece = lax.dynamic_slice_in_dim(x, slot * high, high, 0)
            piece = lax.ppermute(piece, ("row", "col"), self.home_pairs(k))
            at = (own_slot + k - self.row) % self.rows
            out = lax.dynamic_update_slice_in_dim(out, piece, at * wide, 1)
        return out

    def from_home(self, y):
        high = y.shape[0]
        wide = y.shape[1] // self.rows
        out = jnp.zeros((high * self.rows, wide), y.dtype)
        own_slot = (self.row * self.cols + self.col) % self.rows
        for k in range(self.rows):
            at = (own_slot + k - self.row) % self.rows
            piece = lax.dynamic_slice_in_dim(y, at * wide, wide, 1)
            pairs = [(home, first) for first, home in self.home_pairs(k)]
            piece = lax.ppermute(piece, ("row", "col"), pairs)
            slot = (self.row - k) % self.rows
            out = lax.dynamic_update_slice_in_dim(out, piece, slot * high, 0)
        return out

    def ordered(self, mine, other, bit):
        high = (self.group & bit) != 0
        return [jnp.where(high, other, mine), jnp.where(high, mine, other)]


class Weight:
    def __init__(self, place, own, axis):
        self.place, self.own, self.axis = place, own, axis
        size = own.shape[axis] // place.groups
        share, bit = 0, 1
        while bit < place.groups:
            share = 2 * share + jnp.where((place.group & bit) != 0, 1, 0)
            bit *= 2
        self.share = lax.dynamic_slice_in_dim(own, share * size, size, axis)

    def fetch(self):
        steps = range(1, self.place.rows)
        self.parts = [self.place.from_row(self.share, step) for step in steps]
        return self.parts

    def spread(self):
        place = self.place
        bit = place.groups // 2
        while bit > 1:
            self.parts = [
                jnp.concatenate(
                    place.ordered(part, place.swap(part, "dp", bit), bit), axis=self.axis
                )
                for part in self.parts
            ]
            bit //= 2
        return self.parts

    def whole(self):
        place = self.place
        pieces = [self.own]
        for part in self.parts:
            pieces += place.ordered(part, place.swap(part, "dp", 1), 1)
        return jnp.concatenate(pieces, axis=self.axis)


class Summed:
    def __init__(self, place, tall):
        self.place, self.tall = place, tall

    def product(self, tokens, grads):
        place = self.place
        bit = place.group & 1
        blocks = 1 if self.tall else place.rows
        wide = grads.shape[1] // blocks // 2

        def half(which):
            parts = [
                lax.dynamic_slice_in_dim(grads, (2 * i + which) * wide, wide, 1)
                for i in range(blocks)
            ]
            return jnp.concatenate(parts, axis=1) if blocks > 1 else parts[0]

        self.got = place.swap(dot(tokens, half(1 - bit), TN).astype(BF16), "dp", 1)
        self.kept = dot(tokens, half(bit), TN)
        return [self.got, self.kept]

    def across(self):
        rows = self.place.rows
        total = self.kept + self.got.astype(F32)
        axis = 0 if self.tall else 1
        size = total.shape[axis] // rows
        blocks = [lax.slice_in_dim(total, i * size, (i + 1) * size, axis=axis) for i in range(rows)]
        self.got = [
            self.place.to_row(block.astype(BF16), step) for step, block in enumerate(blocks) if step
        ]
        self.kept = blocks[0]
        return self.got

    def along(self):
        place = self.place
        own = self.kept
        for part in self.got:
            own = own + part.astype(F32)
        bit = 2
        while bit < place.groups:
            high = own.shape[0] // 2
            side = jnp.where((place.group & bit) != 0, 1, 0)
            keep = lax.dynamic_slice_in_dim(own, side * high, high, 0)
            send = lax.dynamic_slice_in_dim(own, (1 - side) * high, high, 0)
            own = keep + place.swap(send.astype(BF16), "dp", bit).astype(F32)
            bit *= 2
        self.kept = own.astype(BF16)
        return self.kept

    def back(self):
        place = self.place
        bit = place.groups // 2
        own = self.kept
        while bit > 1:
            own = jnp.concatenate(place.ordered(own, place.swap(own, "dp", bit), bit), axis=0)
            bit //= 2
        self.kept = own
        return own

    def finish(self):
        place = self.place
        return [
            part.astype(F32)
            for part in place.ordered(self.kept, place.swap(self.kept, "dp", 1), 1)
        ]


def gather_tokens(x):
    return lax.all_gather(x, "col", axis=0, tiled=True)


def scatter_tokens(part):
    return lax.psum_scatter(part.astype(BF16), "col", scatter_dimension=0, tiled=True).astype(F32)


def norm_factor(values):
    return lax.rsqrt(jnp.mean(values * values, axis=1, keepdims=True) + EPSILON)


def norm_backward(values, factor, gains, upstream):
    weighted = upstream * gains
    inner = jnp.sum(weighted * values, axis=1, keepdims=True)
    grad_values = factor * weighted - values * (
        factor * factor * factor * inner / values.shape[1]
    )
    return (grad_values, jnp.sum(upstream * values * factor, axis=0))


def body(
    hidden_in,
    seq_lengths,
    gain_attn,
    w_query,
    w_key,
    w_value,
    w_outgate,
    rank_down,
    rank_up,
    decay_bias,
    gain_head,
    w_output,
    gain_ffn,
    w_gate,
    w_up,
    w_down,
    cotangent,
):
    place = Place()
    rows, cols = place.rows, place.cols
    half_rows = SLOT // rows
    home_rows = half_rows // cols
    wide = hidden_in.shape[1]
    rank = rank_down.shape[1]
    head_wide = gain_head.shape[0]
    hidden_wide = w_gate.shape[1]
    value_end = 2 * HEAD_K + HEAD_V

    small = jnp.concatenate([gain_attn, gain_ffn, gain_head, rank_down.reshape(-1)])
    smalls = [small] + [place.from_row(small, step) for step in range(1, rows)]
    home_in = place.to_home(hidden_in)
    residual_in = home_in.astype(F32)
    weight_in = Weight(
        place,
        jnp.concatenate([w_query, w_key, w_value, w_outgate], axis=1),
        0,
    )
    weight_out = Weight(place, w_output, 1)
    weight_down = Weight(place, w_down, 1)
    weight_two = Weight(place, jnp.concatenate([w_gate, w_up], axis=1), 0)
    weight_in.share = after(weight_in.share, home_in)
    got_in = weight_in.fetch()
    home_cot = place.to_home(after(cotangent, home_in))
    for weight in (weight_out, weight_down, weight_two):
        weight.share = after(weight.share, *got_in)
    got_out = weight_out.fetch()
    got_down = weight_down.fetch()
    got_two = weight_two.fetch()
    weight_in.spread()
    w_in = weight_in.whole()

    gain_one = jnp.concatenate([s[:wide] for s in smalls]).astype(F32)
    gain_two = jnp.concatenate([s[wide : 2 * wide] for s in smalls]).astype(F32)
    heads = jnp.stack([s[2 * wide : 2 * wide + head_wide] for s in smalls])
    gain_mix = jnp.roll(heads, place.row, axis=0).reshape(-1).astype(F32)
    w_rank = jnp.concatenate(
        [s[2 * wide + head_wide :].reshape(wide, rank) for s in smalls], axis=0
    )

    place_home = place.row * half_rows + place.col * home_rows
    valid = (place_home + jnp.arange(home_rows) < seq_lengths[0]).astype(F32)[:, None]
    upstream = valid * home_cot.astype(F32)

    factor_one = norm_factor(residual_in)
    normed_one = (residual_in * factor_one * gain_one).astype(BF16)
    tokens_one = gather_tokens(normed_one)
    ffn_grad = gather_tokens(after(upstream.astype(BF16), normed_one))
    tokens_one = after(tokens_one, w_in, upstream, *got_out, *got_down)
    pre = dot(tokens_one, w_in, NN)
    queries = pre[:, :HEAD_K].astype(BF16)
    keys = pre[:, HEAD_K : 2 * HEAD_K].astype(BF16)
    values = pre[:, 2 * HEAD_K : value_end].astype(BF16)
    outgate = pre[:, value_end:]
    rank_mid = dot(tokens_one, w_rank, NN).astype(BF16)
    decay_logits = dot(rank_mid, rank_up, NN) + decay_bias
    decays = jax.nn.log_sigmoid(decay_logits) / 16.0
    decays = after(decays, *got_two)

    ending = attend_state(keys, values, decays)
    steps = [(i, i + 1) for i in range(rows - 1)]
    entry = lax.ppermute(ending.astype(BF16), "row", steps).astype(F32)
    if rows > 2:
        all_fade = jnp.exp(jnp.sum(decays, axis=0))[None, :]
        for _ in range(rows - 2):
            entry = lax.ppermute((entry * all_fade + ending).astype(BF16), "row", steps).astype(F32)
    mixed, faded, states, before = attend_forward(queries, keys, values, decays)
    weight_out.spread()
    spread_down = weight_down.spread()
    spread_two = weight_two.spread()
    w_out = weight_out.whole()
    mixed = after(mixed, w_out)
    mixed = mixed + dot(faded, entry, NT, HIGH)
    factor_head = norm_factor(mixed)
    normed_head = mixed * factor_head * gain_mix
    out_sig = jax.nn.sigmoid(outgate)
    out_act = outgate * out_sig
    gated = (normed_head * out_act).astype(BF16)
    gated = after(gated, ffn_grad, *spread_down, *spread_two)
    attn_out = scatter_tokens(dot(gated, w_out, NN))
    w_ffn = weight_down.whole()
    w_two = weight_two.whole()
    hidden_grad = dot(ffn_grad, w_ffn, NT)
    attn_out = after(attn_out, hidden_grad, w_two)
    residual_mid = residual_in + attn_out

    factor_two = norm_factor(residual_mid)
    normed_two = (residual_mid * factor_two * gain_two).astype(BF16)
    tokens_two = gather_tokens(normed_two)
    both = dot(tokens_two, w_two, NN)
    gate_pre = both[:, :hidden_wide]
    up_pre = both[:, hidden_wide:]
    swish_sig = jax.nn.sigmoid(gate_pre)
    swish_out = gate_pre * swish_sig
    hidden = (swish_out * up_pre).astype(BF16)
    swish_slope = swish_sig * (1.0 + gate_pre * (1.0 - swish_sig))
    gate_grad = (hidden_grad * up_pre * swish_slope).astype(BF16)
    up_grad = (hidden_grad * swish_out).astype(BF16)
    both_grad = jnp.concatenate([gate_grad, up_grad], axis=1)
    normed_two_grad = scatter_tokens(dot(both_grad, w_two, NT))

    sum_two = Summed(place, True)
    sum_down = Summed(place, False)
    held = sum_down.product(hidden, ffn_grad) + sum_two.product(tokens_two, both_grad)
    across_down = sum_down.across()
    across_two = sum_two.across()
    normed_two_grad = after(normed_two_grad, *held)

    mid_part, gain_two_grad = norm_backward(residual_mid, factor_two, gain_two, normed_two_grad)
    mid_grad = upstream + mid_part
    attn_grad = gather_tokens(mid_grad.astype(BF16))
    attn_grad = after(attn_grad, *across_down, *across_two)
    along_down = sum_down.along()
    along_two = sum_two.along()

    gated_grad = dot(attn_grad, w_out, NT)
    ffn_out = scatter_tokens(dot(after(hidden, attn_grad), w_ffn, NN))
    head_grad = gated_grad * out_act
    out_slope = out_sig * (1.0 + outgate * (1.0 - out_sig))
    outgate_grad = (gated_grad * normed_head * out_slope).astype(BF16)
    mixed_grad, gain_mix_grad = norm_backward(mixed, factor_head, gain_mix, head_grad)

    start_grad = dot(mixed_grad, faded, TN, HIGH)
    back = [(i + 1, i) for i in range(rows - 1)]
    exit_grad = lax.ppermute(start_grad.astype(BF16), "row", back).astype(F32)
    if rows > 2:
        for _ in range(rows - 2):
            exit_grad = lax.ppermute(
                (exit_grad * all_fade + start_grad).astype(BF16), "row", back
            ).astype(F32)
    sum_out = Summed(place, False)
    sum_gate = Summed(place, True)
    held = sum_out.product(gated, attn_grad) + sum_gate.product(tokens_one, outgate_grad)
    exit_grad = after(exit_grad, along_down, along_two, *held)
    query_grad, key_grad, value_grad, decay_grad = attend_backward(
        queries, keys, values, decays, mixed_grad, states, before, entry, exit_grad
    )
    across_out = sum_out.across()
    across_gate = sum_gate.across()
    back_down = sum_down.back()
    back_two = sum_two.back()
    in_grad = jnp.concatenate([query_grad, key_grad, value_grad, outgate_grad], axis=1)
    in_grad = after(in_grad, back_down, back_two, *across_out, *across_gate)
    one_part = dot(in_grad, w_in, NT)
    normed_one_grad = scatter_tokens(one_part)

    sums = [Summed(place, True) for _ in range(3)]
    for total, grads in zip(sums, (query_grad, key_grad, value_grad)):
        total.product(tokens_one, after(grads, one_part))
    logit_grad = decay_grad * jax.nn.sigmoid(-decay_logits) / 16.0
    rank_up_part = dot(rank_mid.astype(F32), logit_grad, TN, HIGHEST)
    bias_part = jnp.sum(logit_grad, axis=0)
    rank_term = dot(rank_up.astype(F32), logit_grad, NT, HIGHEST)
    rank_grad = place.sum_over(rank_term, "col").astype(BF16)
    rank_down_part = dot(rank_grad, tokens_one, NN)

    def absolute(x):
        return jnp.roll(x.reshape((rows, -1)), place.row, axis=0).reshape(-1)

    decay_flat = jnp.concatenate(
        [rank_up_part.reshape(-1), bias_part]
        + [absolute(rank_down_part[i]) for i in range(rank)]
    )
    decay_flat = place.sum_over(decay_flat, "dp", "row")

    for total in sums:
        total.across()
    grads_out = []
    for total in (sum_out, sum_gate, *sums):
        total.along()
    for total in (sum_down, sum_two):
        grads_out.append(total.finish())
    for total in (sum_out, sum_gate, *sums):
        total.back()
        grads_out.append(total.finish())
    grad_down, (grad_gate, grad_up), grad_out, grad_og, grad_q, grad_k, grad_v = grads_out
    block_out = place.from_home((valid * (residual_mid + ffn_out)).astype(BF16))

    own_rank = lax.dynamic_slice_in_dim(rank_grad, place.col * home_rows, home_rows, 1)
    normed_one_grad = normed_one_grad + dot(own_rank, w_rank, (((0,), (1,)), ((), ())))
    input_part, gain_one_grad = norm_backward(residual_in, factor_one, gain_one, normed_one_grad)
    grad_input = place.from_home((mid_grad + input_part).astype(BF16)).astype(F32)
    gains = jnp.concatenate([absolute(gain_one_grad), absolute(gain_two_grad), gain_mix_grad])
    gains = place.sum_over(gains, "dp", "row", "col")

    def mine(x):
        size = x.shape[0] // rows
        return lax.dynamic_slice_in_dim(x, place.row * size, size, 0)

    model = wide * rows
    ups = rank * rank_up.shape[1]
    bias_end = ups + decay_bias.shape[0]
    rank_out = decay_flat[bias_end:].reshape(rank, model)
    rank_out = lax.dynamic_slice_in_dim(rank_out, place.row * wide, wide, 1).T

    def columns(pair):
        return jnp.concatenate(pair, axis=1)

    return (
        block_out,
        grad_input,
        mine(gains[:model]),
        columns(grad_q),
        columns(grad_k),
        columns(grad_v),
        columns(grad_og),
        rank_out,
        decay_flat[:ups].reshape(rank, -1),
        decay_flat[ups:bias_end],
        mine(gains[2 * model :]),
        columns(grad_out),
        mine(gains[model : 2 * model]),
        grad_gate,
        grad_up,
        columns(grad_down),
    )


def solution(mesh):
    placed = (
        P(("dp", "col"), "row"),
        P("dp"),
        P("row"),
        P("row", "col"),
        P("row", "col"),
        P("row", "col"),
        P("row", "col"),
        P("row", None),
        P(None, "col"),
        P("col"),
        P("row"),
        P("col", "row"),
        P("row"),
        P("row", "col"),
        P("row", "col"),
        P("col", "row"),
        P(("dp", "col"), "row"),
    )
    return jax.shard_map(
        body,
        mesh=mesh,
        in_specs=placed,
        out_specs=(
            P(("dp", "col"), "row"),
            P(("dp", "col"), "row"),
            P("row"),
            P("row", "col"),
            P("row", "col"),
            P("row", "col"),
            P("row", "col"),
            P("row", None),
            P(None, "col"),
            P("col"),
            P("row"),
            P("col", "row"),
            P("row"),
            P("row", "col"),
            P("row", "col"),
            P("col", "row"),
        ),
        check_vma=False,
    )
```
